256 devices in a mesh: wide: 16 (over y, x), narrow: 16 (over z, core).
Axes of the slice: x: 4, y: 4, z: 8, core: 2. Of those that a mesh axis runs over, the one named last changes fastest.
Arguments:
- charges: bfloat16 [4096, 256, 128], P(('wide', 'narrow')), may hold values from -6 to 6
- pairs_first: int32 [16384, 4], P(('wide', 'narrow')), may hold values from 0 to 15, as said below
- pairs_second: int32 [16384, 4], P(('wide', 'narrow')), may hold values from 0 to 15, as said below
- pairs_third: int32 [16384, 4], P(('wide', 'narrow')), may hold values from 0 to 15, as said below
- matrices_first: bfloat16 [2048, 256, 256], P(('wide', 'narrow')), may hold values from -0.21875 to 0.21875
- matrices_second: bfloat16 [2048, 256, 256], P(('wide', 'narrow')), may hold values from -0.21875 to 0.21875
- matrices_third: bfloat16 [2048, 256, 256], P(('wide', 'narrow')), may hold values from -0.21875 to 0.21875
- box_owner: int32 [16, 16, 16], P('wide', 'narrow'), may hold values from 0 to 15, as said below
Outputs:
- potentials: bfloat16 [4096, 256, 128], P(('wide', 'narrow'))
The draws below stay inside these ranges and needn't reach their ends.
Inputs may be any that keep to these rules, and one draw needn't show every extreme that they name: `pairs_first`: each device's 64 rows hold a source box and a target box below 16, a matrix below 8 and a live flag 0 or 1; live rows come before the others; in every list some device has all rows live. `pairs_second`: same form as pairs_first. `pairs_third`: same form as pairs_first. `box_owner`: for each narrow index, every wide index hands 0 or 2 of its boxes to each owner, and each owner receives exactly 16 boxes.
All inputs are finite; a program needn't handle non-finite values.
Results may differ from the reference program's by a relative error of at most 0.0057.
Values may be sent and summed in bfloat16 or wider, within the bound.
A program may use at most 64 MiB of HBM per device.

```python
import jax
import jax.numpy as jnp
from jax import lax

R = 256
RHS = 128
BOX_DEV = 16
PAIRS = 64
TRANS_DEV = 8
CAP = 2
HOLD = 16
BOXES = 4096
N_WIDE = 16
N_NARROW = 16
DEVICES = 256


def pair_lists(key, salt):
    key = jax.random.fold_in(key, salt)
    keys = jax.random.split(key, 5)
    device_count = N_WIDE * N_NARROW
    sources = jax.random.randint(keys[0], (device_count, PAIRS), 0, BOX_DEV)
    targets = jax.random.randint(keys[1], (device_count, PAIRS), 0, BOX_DEV)
    tables = jax.random.randint(keys[2], (device_count, PAIRS), 0, TRANS_DEV)
    lengths = jax.random.randint(keys[3], (device_count, 1), 2, PAIRS + 1)
    longest = jax.random.randint(keys[4], (), 0, device_count)
    devices = jnp.arange(device_count, dtype=jnp.int32)[:, None]
    lengths = jnp.where(devices == longest, PAIRS, lengths)
    live = (jnp.arange(PAIRS, dtype=jnp.int32)[None, :] < lengths).astype(jnp.int32)
    stacked = jnp.stack([sources, targets, tables, live], axis=-1)
    return stacked.reshape(device_count * PAIRS, 4).astype(jnp.int32)


def draw_pairs_first(key, part):
    return pair_lists(key, 11)


def draw_pairs_second(key, part):
    return pair_lists(key, 23)


def draw_pairs_third(key, part):
    return pair_lists(key, 37)


def draw_box_owner(key, part):
    half = N_WIDE // 2

    def column(narrow_pos):
        column_key = jax.random.fold_in(key, narrow_pos)

        def couple(couple_pos):
            couple_key = jax.random.fold_in(column_key, couple_pos)
            keys = jax.random.split(couple_key, 3)
            order = jax.random.permutation(keys[0], N_WIDE).astype(jnp.int32)
            lower = jnp.repeat(order[:half], CAP)
            upper = jnp.repeat(order[half:], CAP)
            lower = jax.random.permutation(keys[1], lower)
            upper = jax.random.permutation(keys[2], upper)
            return jnp.stack([lower, upper], axis=0)
        rows = jax.vmap(couple)(jnp.arange(half, dtype=jnp.int32))
        return rows.reshape(N_WIDE, BOX_DEV)
    columns = jax.vmap(column)(jnp.arange(N_NARROW, dtype=jnp.int32))
    return jnp.transpose(columns, (1, 0, 2)).astype(jnp.int32)


def block_scale(stream_key, shape, cuts, low, top_value):
    def one(axis_at, parts):
        steps = jax.random.uniform(jax.random.fold_in(jax.random.fold_in(stream_key, 6), axis_at), (parts,), jnp.float32, low / len(cuts), top_value / len(cuts))
        return jnp.repeat(jnp.exp(steps), shape[axis_at] // parts).reshape((-1,) + (1,) * (len(shape) - axis_at - 1))

    level = one(*cuts[0])
    for cut in cuts[1:]:
        level = level * one(*cut)
    return level


def normal_values(stream_key, extent, deviation, most, shards=(), kind=jnp.bfloat16):
    array = deviation * jax.random.normal(stream_key, extent, jnp.float32)
    if shards:
        array = array * block_scale(stream_key, extent, shards, -0.22, 0.18)
    return jnp.clip(array, -most, most).astype(kind)


def setup_inputs(seed: int = 0) -> dict:
    key_of = jax.random.split(jax.random.key(seed), 9)
    return {
        "charges": normal_values(key_of[0], (BOXES, R, RHS), 1.0, 6.0, ((0, 256),)),
        "pairs_first": draw_pairs_first(jax.random.fold_in(key_of[8], 71), 0),
        "pairs_second": draw_pairs_second(jax.random.fold_in(key_of[8], 71), 0),
        "pairs_third": draw_pairs_third(jax.random.fold_in(key_of[8], 71), 0),
        "matrices_first": normal_values(key_of[4], (DEVICES * TRANS_DEV, R, R), (3 * R) ** -0.5, 0.21875, ((0, 256),)),
        "matrices_second": normal_values(key_of[5], (DEVICES * TRANS_DEV, R, R), (3 * R) ** -0.5, 0.21875, ((0, 256),)),
        "matrices_third": normal_values(key_of[6], (DEVICES * TRANS_DEV, R, R), (3 * R) ** -0.5, 0.21875, ((0, 256),)),
        "box_owner": draw_box_owner(jax.random.fold_in(key_of[8], 71), 0),
    }


def translate(coeffs, pairs, mats):
    device_count = coeffs.shape[0] // BOX_DEV
    blocks = coeffs.reshape(device_count, BOX_DEV, R, RHS)
    lists = pairs.reshape(device_count, PAIRS, 4)
    tables = mats.reshape(device_count, TRANS_DEV, R, R)

    def device_level(packed):
        block, listing, table = packed

        def add_pair(running, pair_row):
            matrix = lax.dynamic_index_in_dim(table, pair_row[2], 0, keepdims=False)
            source = lax.dynamic_index_in_dim(block, pair_row[0], 0, keepdims=False)
            product = jnp.dot(matrix, source, preferred_element_type=jnp.float32)
            weight = pair_row[3].astype(jnp.float32)
            return running.at[pair_row[1]].add(weight * product), jnp.zeros((), jnp.float32)

        running, unused = lax.scan(add_pair, jnp.zeros((BOX_DEV, R, RHS), jnp.float32), listing)
        return running.astype(jnp.bfloat16)

    return lax.map(device_level, (blocks, lists, tables)).reshape(coeffs.shape)


def regroup_narrow(coeffs):
    grid = coeffs.reshape(N_WIDE, N_NARROW, BOX_DEV, N_NARROW, R // N_NARROW, RHS)
    grid = jnp.transpose(grid, (0, 3, 2, 1, 4, 5))
    return grid.reshape(coeffs.shape)


def regroup_wide(coeffs):
    grid = coeffs.reshape(N_WIDE, N_NARROW, BOX_DEV, N_WIDE, R // N_WIDE, RHS)
    grid = jnp.transpose(grid, (3, 1, 2, 0, 4, 5))
    return grid.reshape(coeffs.shape)


def handover(final, box_owner):
    grid = final.reshape(N_WIDE, N_NARROW, BOX_DEV, R * RHS)
    flat_count = N_WIDE * BOX_DEV

    def column(narrow_pos):
        boxes = grid[:, narrow_pos].reshape(flat_count, R * RHS)
        owners = box_owner[:, narrow_pos].reshape(flat_count)
        hit = (owners[None, :] == jnp.arange(N_WIDE, dtype=jnp.int32)[:, None]).astype(jnp.int32)
        placed = jnp.cumsum(hit, axis=1) - hit
        slots = jnp.arange(HOLD, dtype=jnp.int32)
        select = hit[:, None, :] * (placed[:, None, :] == slots[None, :, None]).astype(jnp.int32)
        select = select.reshape(N_WIDE * HOLD, flat_count).astype(jnp.bfloat16)
        return jnp.dot(select, boxes, preferred_element_type=jnp.float32).astype(jnp.bfloat16)

    result = lax.map(column, jnp.arange(N_NARROW, dtype=jnp.int32))
    result = result.reshape(N_NARROW, N_WIDE, HOLD, R, RHS)
    result = jnp.transpose(result, (1, 0, 2, 3, 4))
    return result.reshape(N_WIDE * N_NARROW * HOLD, R, RHS)


def reference(charges, pairs_first, pairs_second, pairs_third, matrices_first, matrices_second, matrices_third, box_owner):
    first = translate(charges, pairs_first, matrices_first)
    second = translate(regroup_narrow(first), pairs_second, matrices_second)
    final = translate(regroup_wide(second), pairs_third, matrices_third)
    return handover(final, box_owner)
```

```python
import functools

import jax
import jax.numpy as jnp
from jax import lax
from jax.experimental import pallas as pl
from jax.experimental.pallas import tpu as pltpu
from jax.sharding import PartitionSpec as P

MESH = pl.DeviceIdType.MESH
R = 256
RHS = 128
BOX = 16
PAIRS = 64
TRANS = 8
GROUP = 16
PIECE = R // GROUP
CHUNKS = 2
HALF = RHS // 2
TILES = BOX // 2
UNROLL = 8
BF = jnp.bfloat16
F32 = jnp.float32


def far_first(e):
    return 8 + jnp.where(lax.rem(e, 2) == 1, -((e + 1) // 2), e // 2)


def torus_first(w, e):
    return lax.rem(w + far_first(e), GROUP)


def column_of(row, eye):
    return jnp.sum(jnp.where(eye, row, 0), axis=1, keepdims=True)


def list_table(rows):
    line = lax.broadcasted_iota(jnp.int32, (PAIRS, PAIRS), 0)
    lane = lax.broadcasted_iota(jnp.int32, (PAIRS, PAIRS), 1)
    eye = line == lane
    source, target, matrix, live = (rows[i : i + 1, :] for i in range(4))
    place = lax.broadcasted_iota(jnp.int32, (1, PAIRS), 1)
    group = jnp.where(live > 0, target, BOX)
    key = group * PAIRS + place
    swap = (source ^ target) & 1
    word = (source // 2 + TILES * swap) | (matrix << 4)
    key_col = column_of(key, eye)
    word_col = column_of(word, eye)
    group_col = key_col // PAIRS
    before = key < key_col
    rank_col = jnp.sum(jnp.where(before, 1, 0), axis=1, keepdims=True)
    follows = jnp.sum(jnp.where(before & (group == group_col), 1, 0), axis=1, keepdims=True)
    word_col = word_col | jnp.where((follows > 0) & (group_col < BOX), 1 << 7, 0)
    ordered = jnp.sum(jnp.where(rank_col == lane, word_col, 0), axis=0, keepdims=True)
    upto = jnp.sum(jnp.where(group_col <= lane, 1, 0), axis=0, keepdims=True)
    count = jnp.sum(jnp.where(group_col == lane, 1, 0), axis=0, keepdims=True)
    last = jnp.where(count > 0, upto - 1, PAIRS)
    return ordered, last


def send_table(row):
    line = lax.broadcasted_iota(jnp.int32, (BOX, BOX), 0)
    lane = lax.broadcasted_iota(jnp.int32, (BOX, BOX), 1)
    eye = line == lane
    col = column_of(row, eye)
    earlier = jnp.sum(jnp.where((row == col) & (lane < line), 1, 0), axis=1, keepdims=True)
    slot = 2 * col + earlier
    wide = lax.broadcasted_iota(jnp.int32, (BOX, PAIRS), 1)
    box = lax.broadcasted_iota(jnp.int32, (BOX, PAIRS), 0)
    return jnp.sum(jnp.where(slot == wide, box, 0), axis=0, keepdims=True)


def arrival_table(owners, me):
    hands = jnp.sum(jnp.where(owners == me, 1, 0), axis=1, keepdims=True)
    line = lax.broadcasted_iota(jnp.int32, (GROUP, GROUP), 0)
    lane = lax.broadcasted_iota(jnp.int32, (GROUP, GROUP), 1)
    filled = jnp.where(hands > 0, 1, 0)
    filled_row = jnp.sum(jnp.where(line == lane, filled, 0), axis=0, keepdims=True)
    rank = jnp.sum(jnp.where(lane < line, filled_row, 0), axis=1, keepdims=True)
    wide = lax.broadcasted_iota(jnp.int32, (GROUP, PAIRS), 1)
    index = lax.broadcasted_iota(jnp.int32, (GROUP, PAIRS), 0)
    return jnp.sum(jnp.where((filled > 0) & (rank == wide), index, 0), axis=0, keepdims=True)


def swap_halves(x):
    return pltpu.roll(x, HALF, 1)


def body(
    charges, pairs_a, pairs_b, pairs_c, mats_a, mats_b, mats_c, owner, out,
    c_v, m_a, m_b, m_c, lists, own_in, own_all, tables, table_s,
    x_v, p_v, stage_a, recv_a, stage_b, recv_b, stage_c, recv_c, out_v,
    in_sem, small_sem, table_sem, out_sem, own_send, own_recv, send_sem, recv_sem,
):
    w = lax.axis_index("wide")
    n = lax.axis_index("narrow")
    barrier = pltpu.get_barrier_semaphore()

    def greet(d, carry):
        pl.semaphore_signal(
            barrier, inc=1, device_id=(w, lax.rem(n + d, GROUP)), device_id_type=MESH
        )
        pl.semaphore_signal(
            barrier, inc=1, device_id=(lax.rem(w + d, GROUP), n), device_id_type=MESH
        )
        return carry

    small = [
        pltpu.make_async_copy(src, lists.at[i], small_sem.at[i])
        for i, src in enumerate((pairs_a, pairs_b, pairs_c))
    ]
    small.append(pltpu.make_async_copy(owner, own_in, small_sem.at[3]))
    large = [
        pltpu.make_async_copy(src, dst, in_sem.at[i])
        for i, (src, dst) in enumerate(
            ((charges, c_v), (mats_a, m_a), (mats_b, m_b), (mats_c, m_c))
        )
    ]
    for copy in small:
        copy.start()
    for copy in large:
        copy.start()
    lax.fori_loop(1, GROUP, greet, 0)

    for copy in small:
        copy.wait()
    table_copies = [
        pltpu.make_async_copy(tables.at[i], table_s.at[i], table_sem.at[i]) for i in range(5)
    ]
    for level in range(3):
        ordered, last = list_table(lists[level])
        tables[level, 0:1, 0:PAIRS] = ordered
        tables[level, 1:2, 0:PAIRS] = last
        table_copies[level].start()
    tables[3, 0:1, 0:PAIRS] = send_table(own_in[...])
    table_copies[3].start()
    own_all[w] = jnp.full((8, 128), -1, jnp.int32)
    own_all[w, 0:1, 0:BOX] = own_in[...]
    p_v[PAIRS] = jnp.zeros((R, RHS), BF)
    low = lax.broadcasted_iota(jnp.int32, (R, RHS), 1) < HALF

    def narrow_copy(stage, recv, phase, chunk, d):
        to = lax.rem(n + d, GROUP)
        return pltpu.make_async_remote_copy(
            src_ref=stage.at[chunk, to],
            dst_ref=recv.at[chunk, n],
            send_sem=send_sem.at[phase, chunk, d],
            recv_sem=recv_sem.at[phase, chunk, d],
            device_id=(w, to),
            device_id_type=MESH,
        )

    def wide_copy(stage, recv, phase, chunk, d):
        to = lax.rem(w + d, GROUP)
        return pltpu.make_async_remote_copy(
            src_ref=stage.at[chunk, to],
            dst_ref=recv.at[chunk, w],
            send_sem=send_sem.at[phase, chunk, d],
            recv_sem=recv_sem.at[phase, chunk, d],
            device_id=(to, n),
            device_id_type=MESH,
        )

    copies = {
        0: functools.partial(narrow_copy, stage_a, recv_a, 0),
        1: functools.partial(wide_copy, stage_b, recv_b, 1),
        2: functools.partial(wide_copy, stage_c, recv_c, 2),
    }
    stages = {0: stage_a, 1: stage_b}
    received = {0: recv_a, 1: recv_b, 2: recv_c}

    def owner_copy(d):
        to = lax.rem(w + d, GROUP)
        return pltpu.make_async_remote_copy(
            src_ref=own_all.at[w],
            dst_ref=own_all.at[w],
            send_sem=own_send.at[d],
            recv_sem=own_recv.at[d],
            device_id=(to, n),
            device_id_type=MESH,
        )

    def load_charges(chunk):
        def one(i, carry):
            first = c_v[2 * i].astype(F32)
            second = c_v[2 * i + 1].astype(F32)
            if chunk == 0:
                here = jnp.where(low, first, swap_halves(second))
                there = jnp.where(low, second, swap_halves(first))
            else:
                here = jnp.where(low, swap_halves(first), second)
                there = jnp.where(low, swap_halves(second), first)
            x_v[i] = here.astype(BF)
            x_v[TILES + i] = there.astype(BF)
            return carry

        lax.fori_loop(0, TILES, one, 0)

    def load_received(recv, chunk):
        def one(i, carry):
            tile = recv[chunk, :, i].reshape(R, RHS)
            x_v[i] = tile
            x_v[TILES + i] = swap_halves(tile.astype(F32)).astype(BF)
            return carry

        lax.fori_loop(0, TILES, one, 0)

    def translate(level):
        matrices = (m_a, m_b, m_c)[level]

        def one(r, acc):
            word = table_s[level, 0, r]
            product = jnp.dot(
                matrices[(word >> 4) & 7], x_v[word & 15], preferred_element_type=F32
            )
            acc = jnp.where((word >> 7) & 1 == 1, acc, 0.0) + product
            p_v[r] = acc.astype(BF)
            return acc

        lax.fori_loop(0, PAIRS, one, jnp.zeros((R, RHS), F32), unroll=UNROLL)

    def assemble(level, chunk):
        stage = stages[level]

        def one(i, carry):
            first = p_v[table_s[level, 1, 2 * i]]
            second = p_v[table_s[level, 1, 2 * i + 1]]
            tile = jnp.where(low, first.astype(F32), second.astype(F32)).astype(BF)
            stage[chunk, :, i] = tile.reshape(GROUP, PIECE, RHS)
            return carry

        lax.fori_loop(0, TILES, one, 0)

    def send(level, chunk):
        def one(e, carry):
            copies[level](chunk, far_first(e)).start()
            return carry

        lax.fori_loop(0, GROUP - 1, one, 0)
        me = n if level == 0 else w
        received[level][chunk, me] = stages[level][chunk, me]

    def arrive(level, chunk):
        def one(d, carry):
            copies[level](chunk, d).wait_recv()
            return carry

        lax.fori_loop(1, GROUP, one, 0)

    def sent(level, chunk):
        def one(d, carry):
            copies[level](chunk, d).wait_send()
            return carry

        lax.fori_loop(1, GROUP, one, 0)

    def packet(chunk, to):
        halves = []
        for c in range(2):
            box = table_s[3, 0, 2 * to + c]
            rows = p_v[table_s[2, 1, box]].astype(F32)
            halves.append(jnp.where(box & 1 == c, rows, swap_halves(rows)))
        stage_c[chunk, to] = jnp.where(low, halves[0], halves[1]).astype(BF)

    def hand_over(chunk):
        def one(e, carry):
            d = far_first(e)
            packet(chunk, lax.rem(w + d, GROUP))
            copies[2](chunk, d).start()
            return carry

        lax.fori_loop(0, GROUP - 1, one, 0)
        packet(chunk, w)
        recv_c[chunk, w] = stage_c[chunk, w]

    large[0].wait()
    load_charges(0)
    table_copies[0].wait()
    large[1].wait()
    translate(0)
    assemble(0, 0)
    pl.semaphore_wait(barrier, 2 * (GROUP - 1))
    send(0, 0)

    def give(d, carry):
        owner_copy(d).start()
        return carry

    lax.fori_loop(1, GROUP, give, 0)
    load_charges(1)
    translate(0)
    assemble(0, 1)
    send(0, 1)
    for copy in table_copies[1:4]:
        copy.wait()
    large[2].wait()
    large[3].wait()

    def taken(d, carry):
        owner_copy(d).wait()
        return carry

    lax.fori_loop(1, GROUP, taken, 0)
    tables[4, 0:1, 0:PAIRS] = arrival_table(own_all[:, 0, 0:BOX], w)
    table_copies[4].start()
    table_copies[4].wait()

    arrive(0, 0)
    load_received(recv_a, 0)
    translate(1)
    assemble(1, 0)
    send(1, 0)

    arrive(1, 0)
    load_received(recv_b, 0)
    translate(2)
    hand_over(0)

    arrive(0, 1)
    load_received(recv_a, 1)
    translate(1)
    assemble(1, 1)
    send(1, 1)

    arrive(1, 1)
    load_received(recv_b, 1)
    translate(2)
    hand_over(1)

    for level in range(2):
        for chunk in range(CHUNKS):
            sent(level, chunk)
    arrive(2, 0)
    arrive(2, 1)

    def place(j):
        return pltpu.make_async_copy(
            out_v.at[pl.ds(2 * j, 2)], out.at[pl.ds(2 * j, 2)], out_sem.at[j]
        )

    def finish(j, carry):
        origin = table_s[4, 0, j]
        left = recv_c[0, origin].astype(F32)
        right = recv_c[1, origin].astype(F32)
        out_v[2 * j] = jnp.where(low, left, swap_halves(right)).astype(BF)
        out_v[2 * j + 1] = jnp.where(low, swap_halves(left), right).astype(BF)
        place(j).start()
        return carry

    lax.fori_loop(0, TILES, finish, 0)

    def placed(j, carry):
        place(j).wait()
        return carry

    lax.fori_loop(0, TILES, placed, 0)
    for chunk in range(CHUNKS):
        sent(2, chunk)


def per_device(charges, pairs_a, pairs_b, pairs_c, mats_a, mats_b, mats_c, box_owner):
    any_space = pl.BlockSpec(memory_space=pl.ANY)
    flops = 2 * 3 * PAIRS * R * R * RHS
    return pl.pallas_call(
        body,
        out_shape=jax.ShapeDtypeStruct(charges.shape, charges.dtype),
        in_specs=[any_space] * 8,
        out_specs=any_space,
        scratch_shapes=[
            pltpu.VMEM((BOX, R, RHS), BF),
            *[pltpu.VMEM((TRANS, R, R), BF)] * 3,
            pltpu.VMEM((3, 4, PAIRS), jnp.int32),
            pltpu.VMEM((1, BOX), jnp.int32),
            pltpu.VMEM((GROUP, 8, 128), jnp.int32),
            pltpu.VMEM((5, 8, 128), jnp.int32),
            pltpu.SMEM((5, 8, 128), jnp.int32),
            pltpu.VMEM((2 * TILES, R, RHS), BF),
            pltpu.VMEM((PAIRS + 1, R, RHS), BF),
            pltpu.VMEM((CHUNKS, GROUP, TILES, PIECE, RHS), BF),
            pltpu.VMEM((CHUNKS, GROUP, TILES, PIECE, RHS), BF),
            pltpu.VMEM((CHUNKS, GROUP, TILES, PIECE, RHS), BF),
            pltpu.VMEM((CHUNKS, GROUP, TILES, PIECE, RHS), BF),
            pltpu.VMEM((CHUNKS, GROUP, R, RHS), BF),
            pltpu.VMEM((CHUNKS, GROUP, R, RHS), BF),
            pltpu.VMEM((BOX, R, RHS), BF),
            pltpu.SemaphoreType.DMA((4,)),
            pltpu.SemaphoreType.DMA((4,)),
            pltpu.SemaphoreType.DMA((5,)),
            pltpu.SemaphoreType.DMA((TILES,)),
            pltpu.SemaphoreType.DMA((GROUP,)),
            pltpu.SemaphoreType.DMA((GROUP,)),
            pltpu.SemaphoreType.DMA((3, CHUNKS, GROUP)),
            pltpu.SemaphoreType.DMA((3, CHUNKS, GROUP)),
        ],
        compiler_params=pltpu.CompilerParams(
            collective_id=0, has_side_effects=True, vmem_limit_bytes=48 << 20
        ),
        cost_estimate=pl.CostEstimate(flops=flops, bytes_accessed=5 << 20, transcendentals=0),
        name="butterfly",
    )(
        charges,
        pairs_a.T,
        pairs_b.T,
        pairs_c.T,
        mats_a,
        mats_b,
        mats_c,
        box_owner.reshape(1, BOX),
    )


def solution(mesh):
    both = ("wide", "narrow")
    placed = (
        P(both, None, None),
        P(both, None),
        P(both, None),
        P(both, None),
        P(both, None, None),
        P(both, None, None),
        P(both, None, None),
        P("wide", "narrow", None),
    )
    return jax.shard_map(
        per_device,
        mesh=mesh,
        in_specs=placed,
        out_specs=P(both, None, None),
        check_vma=False,
    )
```

```python
import functools

import jax
import jax.numpy as jnp
from jax import lax
from jax.experimental import pallas as pl
from jax.experimental.pallas import tpu as pltpu
from jax.sharding import PartitionSpec as P

MESH = pl.DeviceIdType.MESH
R = 256
RHS = 128
BOX = 16
PAIRS = 64
TRANS = 8
GROUP = 16
PIECE = R // GROUP
CHUNKS = 4
LANES = RHS // CHUNKS
TILES = BOX // CHUNKS
PARTS = CHUNKS // 2
ROWS = R // PARTS
PAIRS_OUT = BOX // 2
SPLIT = 4
UNROLL = 32
BF = jnp.bfloat16
F32 = jnp.float32


def far_first(e):
    return 8 + jnp.where(lax.rem(e, 2) == 1, -((e + 1) // 2), e // 2)


def column_of(row, eye):
    return jnp.sum(jnp.where(eye, row, 0), axis=1, keepdims=True)


def list_table(rows, tiled):
    line = lax.broadcasted_iota(jnp.int32, (PAIRS, PAIRS), 0)
    lane = lax.broadcasted_iota(jnp.int32, (PAIRS, PAIRS), 1)
    eye = line == lane
    source, target, matrix, live = (rows[i : i + 1, :] for i in range(4))
    place = lax.broadcasted_iota(jnp.int32, (1, PAIRS), 1)
    group = jnp.where(live > 0, target, BOX)
    key = group * PAIRS + place
    turn = (target - source) & (CHUNKS - 1)
    place_of = source // CHUNKS + TILES * turn if tiled else source
    word = place_of | (matrix << 4)
    key_col = column_of(key, eye)
    word_col = column_of(word, eye)
    group_col = key_col // PAIRS
    before = key < key_col
    rank_col = jnp.sum(jnp.where(before, 1, 0), axis=1, keepdims=True)
    follows = jnp.sum(jnp.where(before & (group == group_col), 1, 0), axis=1, keepdims=True)
    word_col = word_col | jnp.where((follows > 0) & (group_col < BOX), 1 << 7, 0)
    ordered = jnp.sum(jnp.where(rank_col == lane, word_col, 0), axis=0, keepdims=True)
    upto = jnp.sum(jnp.where(group_col <= lane, 1, 0), axis=0, keepdims=True)
    count = jnp.sum(jnp.where(group_col == lane, 1, 0), axis=0, keepdims=True)
    last = jnp.where(count > 0, upto - 1, PAIRS)
    return ordered, last


def send_table(row):
    line = lax.broadcasted_iota(jnp.int32, (BOX, BOX), 0)
    lane = lax.broadcasted_iota(jnp.int32, (BOX, BOX), 1)
    eye = line == lane
    col = column_of(row, eye)
    earlier = jnp.sum(jnp.where((row == col) & (lane < line), 1, 0), axis=1, keepdims=True)
    slot = 2 * col + earlier
    wide = lax.broadcasted_iota(jnp.int32, (BOX, PAIRS), 1)
    box = lax.broadcasted_iota(jnp.int32, (BOX, PAIRS), 0)
    return jnp.sum(jnp.where(slot == wide, box, 0), axis=0, keepdims=True)


def arrival_table(owners, me):
    hands = jnp.sum(jnp.where(owners == me, 1, 0), axis=1, keepdims=True)
    line = lax.broadcasted_iota(jnp.int32, (GROUP, GROUP), 0)
    lane = lax.broadcasted_iota(jnp.int32, (GROUP, GROUP), 1)
    filled = jnp.where(hands > 0, 1, 0)
    filled_row = jnp.sum(jnp.where(line == lane, filled, 0), axis=0, keepdims=True)
    rank = jnp.sum(jnp.where(lane < line, filled_row, 0), axis=1, keepdims=True)
    wide = lax.broadcasted_iota(jnp.int32, (GROUP, PAIRS), 1)
    index = lax.broadcasted_iota(jnp.int32, (GROUP, PAIRS), 0)
    return jnp.sum(jnp.where((filled > 0) & (rank == wide), index, 0), axis=0, keepdims=True)


def turned(x, groups):
    if isinstance(groups, int):
        return x if groups % CHUNKS == 0 else pltpu.roll(x, (groups % CHUNKS) * LANES, 1)
    return pltpu.roll(x, (groups & (CHUNKS - 1)) * LANES, 1)


def body(
    charges, pairs_a, pairs_b, pairs_c, mats_a, mats_b, mats_c, owner, out,
    c_v, m_a, m_b, m_c, lists, own_in, own_all, tables, table_s, arrival_s,
    x_v, p_v, stage_a, recv_a, stage_b, recv_b, stage_c, *rest,
):
    recv_c = rest[:CHUNKS]
    out_v, in_sem, late_sem, small_sem, table_sem, out_sem, own_send, own_recv, send_sem, recv_sem = rest[CHUNKS:]
    w = lax.axis_index("wide")
    n = lax.axis_index("narrow")
    barrier = pltpu.get_barrier_semaphore()

    def greet(d, carry):
        pl.semaphore_signal(
            barrier, inc=1, device_id=(w, lax.rem(n + d, GROUP)), device_id_type=MESH
        )
        pl.semaphore_signal(
            barrier, inc=1, device_id=(lax.rem(w + d, GROUP), n), device_id_type=MESH
        )
        return carry

    small = [
        pltpu.make_async_copy(src, lists.at[i], small_sem.at[i])
        for i, src in enumerate((pairs_a, pairs_b, pairs_c))
    ]
    small.append(pltpu.make_async_copy(owner, own_in, small_sem.at[3]))
    first_in = []
    for i, (src, dst) in enumerate(((charges, c_v), (mats_a, m_a))):
        size = src.shape[0] // SPLIT
        for k in range(SPLIT):
            span = pl.ds(k * size, size)
            first_in.append(
                pltpu.make_async_copy(src.at[span], dst.at[span], in_sem.at[i, k])
            )
    late_in = [
        pltpu.make_async_copy(mats_b, m_b, late_sem.at[0]),
        pltpu.make_async_copy(mats_c, m_c, late_sem.at[1]),
    ]
    for copy in small:
        copy.start()
    for copy in first_in:
        copy.start()
    lax.fori_loop(1, GROUP, greet, 0)

    table_copies = [
        pltpu.make_async_copy(tables.at[i], table_s.at[i], table_sem.at[i]) for i in range(4)
    ]
    arrival_copy = pltpu.make_async_copy(tables.at[4], arrival_s, table_sem.at[4])
    for copy in small:
        copy.wait()

    def list_of(level):
        ordered, last = list_table(lists[level], level > 0)
        tables[level, 0:1, 0:PAIRS] = ordered
        tables[level, 1:2, 0:PAIRS] = last
        table_copies[level].start()

    list_of(0)
    list_of(1)
    list_of(2)
    tables[3, 0:1, 0:PAIRS] = send_table(own_in[...])
    table_copies[3].start()
    own_all[w] = jnp.full((8, 128), -1, jnp.int32)
    own_all[w, 0:1, 0:BOX] = own_in[...]
    p_v[PAIRS] = jnp.zeros((R, RHS), BF)
    group = lax.broadcasted_iota(jnp.int32, (R, RHS), 1) // LANES

    def side_by_side(parts):
        tile = parts[0]
        for g in range(1, CHUNKS):
            tile = jnp.where(group[: tile.shape[0]] == g, parts[g], tile)
        return tile

    def narrow_copy(chunk, d):
        to = lax.rem(n + d, GROUP)
        return pltpu.make_async_remote_copy(
            src_ref=stage_a.at[chunk, to],
            dst_ref=recv_a.at[chunk, n],
            send_sem=send_sem.at[0, chunk, d],
            recv_sem=recv_sem.at[0, chunk, d],
            device_id=(w, to),
            device_id_type=MESH,
        )

    def wide_copy(phase, chunk, d):
        to = lax.rem(w + d, GROUP)
        stage, recv = ((stage_b, recv_b.at[chunk]), (stage_c, recv_c[chunk]))[phase - 1]
        return pltpu.make_async_remote_copy(
            src_ref=stage.at[chunk, to],
            dst_ref=recv.at[w],
            send_sem=send_sem.at[phase, chunk, d],
            recv_sem=recv_sem.at[phase, chunk, d],
            device_id=(to, n),
            device_id_type=MESH,
        )

    copies = (
        narrow_copy,
        functools.partial(wide_copy, 1),
        functools.partial(wide_copy, 2),
    )

    def owner_copy(d):
        to = lax.rem(w + d, GROUP)
        return pltpu.make_async_remote_copy(
            src_ref=own_all.at[w],
            dst_ref=own_all.at[w],
            send_sem=own_send.at[d],
            recv_sem=own_recv.at[d],
            device_id=(to, n),
            device_id_type=MESH,
        )

    def loop(low, high, step):
        def one(i, carry):
            step(i)
            return carry

        lax.fori_loop(low, high, one, 0)

    def load_received(recv, chunk):
        def step(i):
            tile = recv[chunk, :, i].reshape(R, RHS)
            for v in range(CHUNKS):
                x_v[v * TILES + i] = turned(tile, v)

        loop(0, TILES, step)

    def translate(level):
        matrices = (m_a, m_b, m_c)[level]
        sources = c_v if level == 0 else x_v

        def one(r, acc):
            word = table_s[level, 0, r]
            product = jnp.dot(
                matrices[(word >> 4) & 7], sources[word & 15], preferred_element_type=F32
            )
            acc = jnp.where((word >> 7) & 1 == 1, acc, 0.0) + product
            p_v[r] = acc.astype(BF)
            return acc

        lax.fori_loop(0, PAIRS, one, jnp.zeros((R, RHS), F32), unroll=UNROLL)

    def assemble(level, chunk):
        stage = (stage_a, stage_b)[level]

        def step(i):
            parts = []
            for g in range(CHUNKS):
                box = p_v[table_s[level, 1, CHUNKS * i + g]]
                parts.append(turned(box, g - chunk) if level == 0 else box)
            stage[chunk, :, i] = side_by_side(parts).reshape(GROUP, PIECE, RHS)

        loop(0, TILES, step)

    def send(level, chunk):
        loop(0, GROUP - 1, lambda e: copies[level](chunk, far_first(e)).start())
        if level == 0:
            recv_a[chunk, n] = stage_a[chunk, n]
        else:
            recv_b[chunk, w] = stage_b[chunk, w]

    def arrive(level, chunk):
        loop(1, GROUP, lambda d: copies[level](chunk, d).wait_recv())

    def sent(level, chunk):
        loop(1, GROUP, lambda d: copies[level](chunk, d).wait_send())

    def packet(chunk, to):
        parts = []
        for c in range(2):
            box = table_s[3, 0, 2 * to + c]
            slot = table_s[2, 1, box]
            for r in range(PARTS):
                rows = p_v[slot, r * ROWS : (r + 1) * ROWS]
                parts.append(turned(rows, c * PARTS + r - box))
        stage_c[chunk, to] = side_by_side(parts)

    def hand(chunk, low, high, pack=True, start=True):
        def step(e):
            d = far_first(e)
            if pack:
                packet(chunk, lax.rem(w + d, GROUP))
            if start:
                copies[2](chunk, d).start()

        loop(low, high, step)

    def keep(chunk):
        packet(chunk, w)
        recv_c[chunk][w] = stage_c[chunk, w]

    def place(j):
        span = pl.ds(2 * j, 2)
        return pltpu.make_async_copy(out_v.at[span], out.at[span], out_sem.at[j])

    def finish(chunk):
        def step(j):
            packed = recv_c[chunk][arrival_s[0, j]]
            lanes = slice(chunk * LANES, (chunk + 1) * LANES)
            for c in range(2):
                for r in range(PARTS):
                    rows = turned(packed, chunk - (c * PARTS + r))
                    out_v[2 * j + c, r * ROWS : (r + 1) * ROWS, lanes] = rows[:, lanes]
            if chunk == CHUNKS - 1:
                place(j).start()

        loop(0, PAIRS_OUT, step)

    def level_two(chunk):
        load_received(recv_a, chunk)
        translate(1)
        assemble(1, chunk)
        send(1, chunk)

    def level_three(chunk):
        load_received(recv_b, chunk)
        translate(2)

    table_copies[0].wait()
    for copy in first_in:
        copy.wait()
    for copy in late_in:
        copy.start()
    translate(0)
    assemble(0, 0)
    pl.semaphore_wait(barrier, 2 * (GROUP - 1))
    send(0, 0)
    loop(1, GROUP, lambda d: owner_copy(d).start())
    for chunk in range(1, CHUNKS):
        assemble(0, chunk)
    for copy in table_copies[1:4]:
        copy.wait()
    for copy in late_in:
        copy.wait()
    loop(1, GROUP, lambda d: owner_copy(d).wait())
    tables[4, 0:1, 0:PAIRS] = arrival_table(own_all[:, 0, 0:BOX], w)
    arrival_copy.start()
    arrival_copy.wait()

    arrive(0, 0)
    send(0, 1)
    level_two(0)
    arrive(0, 1)
    send(0, 2)
    level_two(1)
    arrive(1, 0)
    level_three(0)
    hand(0, 0, 15)
    keep(0)
    arrive(0, 2)
    send(0, 3)
    level_two(2)
    arrive(1, 1)
    level_three(1)
    hand(1, 0, 7)
    hand(1, 7, 15, start=False)
    keep(1)
    arrive(0, 3)
    level_two(3)
    hand(1, 7, 15, pack=False)
    arrive(1, 2)
    level_three(2)
    hand(2, 0, 7)
    hand(2, 7, 15, start=False)
    keep(2)
    arrive(1, 3)
    hand(2, 7, 15, pack=False)
    level_three(3)
    hand(3, 0, 15)
    keep(3)

    for level in range(2):
        for chunk in range(CHUNKS):
            sent(level, chunk)
    for chunk in range(CHUNKS):
        arrive(2, chunk)
        finish(chunk)
    loop(0, PAIRS_OUT, lambda j: place(j).wait())
    for chunk in range(CHUNKS):
        sent(2, chunk)


def per_device(charges, pairs_a, pairs_b, pairs_c, mats_a, mats_b, mats_c, box_owner):
    in_hbm = pl.BlockSpec(memory_space=pltpu.HBM)
    flops = 2 * 3 * PAIRS * R * R * RHS
    return pl.pallas_call(
        body,
        out_shape=jax.ShapeDtypeStruct(charges.shape, charges.dtype),
        in_specs=[in_hbm] * 8,
        out_specs=in_hbm,
        scratch_shapes=[
            pltpu.VMEM((BOX, R, RHS), BF),
            *[pltpu.VMEM((TRANS, R, R), BF)] * 3,
            pltpu.VMEM((3, 4, PAIRS), jnp.int32),
            pltpu.VMEM((1, BOX), jnp.int32),
            pltpu.VMEM((GROUP, 8, 128), jnp.int32),
            pltpu.VMEM((5, 8, 128), jnp.int32),
            pltpu.SMEM((4, 8, 128), jnp.int32),
            pltpu.SMEM((8, 128), jnp.int32),
            pltpu.VMEM((BOX, R, RHS), BF),
            pltpu.VMEM((PAIRS + 1, R, RHS), BF),
            *[pltpu.VMEM((CHUNKS, GROUP, TILES, PIECE, RHS), BF)] * 4,
            pltpu.VMEM((CHUNKS, GROUP, ROWS, RHS), BF),
            *[pltpu.VMEM((GROUP, ROWS, RHS), BF)] * CHUNKS,
            pltpu.VMEM((BOX, R, RHS), BF),
            pltpu.SemaphoreType.DMA((2, SPLIT)),
            pltpu.SemaphoreType.DMA((2,)),
            pltpu.SemaphoreType.DMA((4,)),
            pltpu.SemaphoreType.DMA((5,)),
            pltpu.SemaphoreType.DMA((PAIRS_OUT,)),
            pltpu.SemaphoreType.DMA((GROUP,)),
            pltpu.SemaphoreType.DMA((GROUP,)),
            pltpu.SemaphoreType.DMA((3, CHUNKS, GROUP)),
            pltpu.SemaphoreType.DMA((3, CHUNKS, GROUP)),
        ],
        compiler_params=pltpu.CompilerParams(
            collective_id=0, has_side_effects=True, vmem_limit_bytes=62 << 20
        ),
        cost_estimate=pl.CostEstimate(flops=flops, bytes_accessed=5 << 20, transcendentals=0),
        name="butterfly",
    )(
        charges,
        pairs_a.T,
        pairs_b.T,
        pairs_c.T,
        mats_a,
        mats_b,
        mats_c,
        box_owner.reshape(1, BOX),
    )


def solution(mesh):
    both = ("wide", "narrow")
    placed = (
        P(both, None, None),
        P(both, None),
        P(both, None),
        P(both, None),
        P(both, None, None),
        P(both, None, None),
        P(both, None, None),
        P("wide", "narrow", None),
    )
    return jax.shard_map(
        per_device,
        mesh=mesh,
        in_specs=placed,
        out_specs=P(both, None, None),
        check_vma=False,
    )
```

```python
import functools

import jax
import jax.numpy as jnp
from jax import lax
from jax.experimental import pallas as pl
from jax.experimental.pallas import tpu as pltpu
from jax.sharding import PartitionSpec as P

MESH = pl.DeviceIdType.MESH
R = 256
RHS = 128
BOX = 16
PAIRS = 64
TRANS = 8
GROUP = 16
PIECE = R // GROUP
CHUNKS = 4
LANES = RHS // CHUNKS
TILES = BOX // CHUNKS
PARTS = CHUNKS // 2
ROWS = R // PARTS
PAIRS_OUT = BOX // 2
SPLIT = 4
UNROLL = 32
BF = jnp.bfloat16
F32 = jnp.float32


def far_first(e):
    return 8 + jnp.where(lax.rem(e, 2) == 1, -((e + 1) // 2), e // 2)


NEAR = tuple(
    4 * dy + dx
    for dy, dx in (
        (0, 1), (0, 3), (1, 0), (3, 0), (0, 2), (2, 0), (1, 1), (3, 3),
        (1, 3), (3, 1), (1, 2), (3, 2), (2, 1), (2, 3), (2, 2),
    )
)


def listed(order, e):
    low = sum(d << (4 * i) for i, d in enumerate(order[:7]))
    high = sum(d << (4 * i) for i, d in enumerate(order[7:14]))
    first = (jnp.int32(low) >> (4 * jnp.minimum(e, 6))) & 15
    later = (jnp.int32(high) >> (4 * jnp.clip(e - 7, 0, 6))) & 15
    return jnp.where(e < 7, first, jnp.where(e < 14, later, order[14]))


def on_torus(w, d):
    return ((w // 4 + d // 4) & 3) * 4 + ((w + d) & 3)


def column_of(row, eye):
    return jnp.sum(jnp.where(eye, row, 0), axis=1, keepdims=True)


def list_table(rows, tiled):
    line = lax.broadcasted_iota(jnp.int32, (PAIRS, PAIRS), 0)
    lane = lax.broadcasted_iota(jnp.int32, (PAIRS, PAIRS), 1)
    eye = line == lane
    source, target, matrix, live = (rows[i : i + 1, :] for i in range(4))
    place = lax.broadcasted_iota(jnp.int32, (1, PAIRS), 1)
    group = jnp.where(live > 0, target, BOX)
    key = group * PAIRS + place
    turn = (target - source) & (CHUNKS - 1)
    place_of = source // CHUNKS + TILES * turn if tiled else source
    word = place_of | (matrix << 4)
    key_col = column_of(key, eye)
    word_col = column_of(word, eye)
    group_col = key_col // PAIRS
    before = key < key_col
    rank_col = jnp.sum(jnp.where(before, 1, 0), axis=1, keepdims=True)
    follows = jnp.sum(jnp.where(before & (group == group_col), 1, 0), axis=1, keepdims=True)
    word_col = word_col | jnp.where((follows > 0) & (group_col < BOX), 1 << 7, 0)
    ordered = jnp.sum(jnp.where(rank_col == lane, word_col, 0), axis=0, keepdims=True)
    upto = jnp.sum(jnp.where(group_col <= lane, 1, 0), axis=0, keepdims=True)
    count = jnp.sum(jnp.where(group_col == lane, 1, 0), axis=0, keepdims=True)
    last = jnp.where(count > 0, upto - 1, PAIRS)
    return ordered, last


def send_table(row):
    line = lax.broadcasted_iota(jnp.int32, (BOX, BOX), 0)
    lane = lax.broadcasted_iota(jnp.int32, (BOX, BOX), 1)
    eye = line == lane
    col = column_of(row, eye)
    earlier = jnp.sum(jnp.where((row == col) & (lane < line), 1, 0), axis=1, keepdims=True)
    slot = 2 * col + earlier
    wide = lax.broadcasted_iota(jnp.int32, (BOX, PAIRS), 1)
    box = lax.broadcasted_iota(jnp.int32, (BOX, PAIRS), 0)
    return jnp.sum(jnp.where(slot == wide, box, 0), axis=0, keepdims=True)


def arrival_table(owners, me):
    hands = jnp.sum(jnp.where(owners == me, 1, 0), axis=1, keepdims=True)
    line = lax.broadcasted_iota(jnp.int32, (GROUP, GROUP), 0)
    lane = lax.broadcasted_iota(jnp.int32, (GROUP, GROUP), 1)
    filled = jnp.where(hands > 0, 1, 0)
    filled_row = jnp.sum(jnp.where(line == lane, filled, 0), axis=0, keepdims=True)
    rank = jnp.sum(jnp.where(lane < line, filled_row, 0), axis=1, keepdims=True)
    wide = lax.broadcasted_iota(jnp.int32, (GROUP, PAIRS), 1)
    index = lax.broadcasted_iota(jnp.int32, (GROUP, PAIRS), 0)
    return jnp.sum(jnp.where((filled > 0) & (rank == wide), index, 0), axis=0, keepdims=True)


def turned(x, groups):
    if isinstance(groups, int):
        return x if groups % CHUNKS == 0 else pltpu.roll(x, (groups % CHUNKS) * LANES, 1)
    return pltpu.roll(x, (groups & (CHUNKS - 1)) * LANES, 1)


def body(
    charges, pairs_a, pairs_b, pairs_c, mats_a, mats_b, mats_c, owner, out,
    c_v, m_a, m_b, m_c, lists, own_in, own_all, tables, table_s, arrival_s,
    x_v, p_v, stage_a, recv_a, stage_b, recv_b, stage_c, *rest,
):
    recv_c = rest[:CHUNKS]
    out_v, in_sem, late_sem, small_sem, table_sem, out_sem, own_send, own_recv, send_sem, recv_sem = rest[CHUNKS:]
    w = lax.axis_index("wide")
    n = lax.axis_index("narrow")
    barrier = pltpu.get_barrier_semaphore()

    def greet(d, carry):
        pl.semaphore_signal(
            barrier, inc=1, device_id=(w, lax.rem(n + d, GROUP)), device_id_type=MESH
        )
        pl.semaphore_signal(
            barrier, inc=1, device_id=(lax.rem(w + d, GROUP), n), device_id_type=MESH
        )
        return carry

    small = [
        pltpu.make_async_copy(src, lists.at[i], small_sem.at[i])
        for i, src in enumerate((pairs_a, pairs_b, pairs_c))
    ]
    small.append(pltpu.make_async_copy(owner, own_in, small_sem.at[3]))
    first_in = []
    for i, (src, dst) in enumerate(((charges, c_v), (mats_a, m_a))):
        size = src.shape[0] // SPLIT
        for k in range(SPLIT):
            span = pl.ds(k * size, size)
            first_in.append(
                pltpu.make_async_copy(src.at[span], dst.at[span], in_sem.at[i, k])
            )
    late_in = [
        pltpu.make_async_copy(mats_b, m_b, late_sem.at[0]),
        pltpu.make_async_copy(mats_c, m_c, late_sem.at[1]),
    ]
    for copy in small:
        copy.start()
    for copy in first_in:
        copy.start()
    lax.fori_loop(1, GROUP, greet, 0)

    table_copies = [
        pltpu.make_async_copy(tables.at[i], table_s.at[i], table_sem.at[i]) for i in range(4)
    ]
    arrival_copy = pltpu.make_async_copy(tables.at[4], arrival_s, table_sem.at[4])
    for copy in small:
        copy.wait()

    def list_of(level):
        ordered, last = list_table(lists[level], level > 0)
        tables[level, 0:1, 0:PAIRS] = ordered
        tables[level, 1:2, 0:PAIRS] = last
        table_copies[level].start()

    list_of(0)
    own_all[w] = jnp.full((8, 128), -1, jnp.int32)
    own_all[w, 0:1, 0:BOX] = own_in[...]
    p_v[PAIRS] = jnp.zeros((R, RHS), BF)
    group = lax.broadcasted_iota(jnp.int32, (R, RHS), 1) // LANES

    def side_by_side(parts):
        tile = parts[0]
        for g in range(1, CHUNKS):
            tile = jnp.where(group[: tile.shape[0]] == g, parts[g], tile)
        return tile

    def narrow_copy(chunk, d):
        to = lax.rem(n + d, GROUP)
        return pltpu.make_async_remote_copy(
            src_ref=stage_a.at[chunk, to],
            dst_ref=recv_a.at[chunk, n],
            send_sem=send_sem.at[0, chunk, d],
            recv_sem=recv_sem.at[0, chunk, d],
            device_id=(w, to),
            device_id_type=MESH,
        )

    def wide_copy(phase, chunk, d):
        to = on_torus(w, d)
        stage, recv = ((stage_b, recv_b.at[chunk]), (stage_c, recv_c[chunk]))[phase - 1]
        return pltpu.make_async_remote_copy(
            src_ref=stage.at[chunk, to],
            dst_ref=recv.at[w],
            send_sem=send_sem.at[phase, chunk, d],
            recv_sem=recv_sem.at[phase, chunk, d],
            device_id=(to, n),
            device_id_type=MESH,
        )

    copies = (
        narrow_copy,
        functools.partial(wide_copy, 1),
        functools.partial(wide_copy, 2),
    )

    def owner_copy(d):
        to = lax.rem(w + d, GROUP)
        return pltpu.make_async_remote_copy(
            src_ref=own_all.at[w],
            dst_ref=own_all.at[w],
            send_sem=own_send.at[d],
            recv_sem=own_recv.at[d],
            device_id=(to, n),
            device_id_type=MESH,
        )

    def loop(low, high, step):
        def one(i, carry):
            step(i)
            return carry

        lax.fori_loop(low, high, one, 0)

    def load_received(recv, chunk):
        def step(i):
            tile = recv[chunk, :, i].reshape(R, RHS)
            for v in range(CHUNKS):
                x_v[v * TILES + i] = turned(tile, v)

        loop(0, TILES, step)

    def translate(level):
        matrices = (m_a, m_b, m_c)[level]
        sources = c_v if level == 0 else x_v

        def one(r, acc):
            word = table_s[level, 0, r]
            product = jnp.dot(
                matrices[(word >> 4) & 7], sources[word & 15], preferred_element_type=F32
            )
            acc = jnp.where((word >> 7) & 1 == 1, acc, 0.0) + product
            p_v[r] = acc.astype(BF)
            return acc

        lax.fori_loop(0, PAIRS, one, jnp.zeros((R, RHS), F32), unroll=UNROLL)

    def assemble(level, chunk):
        stage = (stage_a, stage_b)[level]

        def step(i):
            parts = []
            for g in range(CHUNKS):
                box = p_v[table_s[level, 1, CHUNKS * i + g]]
                parts.append(turned(box, g - chunk) if level == 0 else box)
            stage[chunk, :, i] = side_by_side(parts).reshape(GROUP, PIECE, RHS)

        loop(0, TILES, step)

    def send(level, chunk):
        loop(0, GROUP - 1, lambda e: copies[level](chunk, far_first(e) if level == 0 else listed(NEAR[::-1], e)).start())
        if level == 0:
            recv_a[chunk, n] = stage_a[chunk, n]
        else:
            recv_b[chunk, w] = stage_b[chunk, w]

    def arrive(level, chunk):
        loop(1, GROUP, lambda d: copies[level](chunk, d).wait_recv())

    def sent(level, chunk):
        loop(1, GROUP, lambda d: copies[level](chunk, d).wait_send())

    def packet(chunk, to):
        parts = []
        for c in range(2):
            box = table_s[3, 0, 2 * to + c]
            slot = table_s[2, 1, box]
            for r in range(PARTS):
                rows = p_v[slot, r * ROWS : (r + 1) * ROWS]
                parts.append(turned(rows, c * PARTS + r - box))
        stage_c[chunk, to] = side_by_side(parts)

    def hand(chunk, low, high, pack=True, start=True):
        def step(e):
            d = listed(NEAR[::-1], e)
            if pack:
                packet(chunk, on_torus(w, d))
            if start:
                copies[2](chunk, d).start()

        loop(low, high, step)

    def keep(chunk):
        packet(chunk, w)
        recv_c[chunk][w] = stage_c[chunk, w]

    def place(j):
        span = pl.ds(2 * j, 2)
        return pltpu.make_async_copy(out_v.at[span], out.at[span], out_sem.at[j])

    def finish(chunk):
        def step(j):
            packed = recv_c[chunk][arrival_s[0, j]]
            lanes = slice(chunk * LANES, (chunk + 1) * LANES)
            for c in range(2):
                for r in range(PARTS):
                    rows = turned(packed, chunk - (c * PARTS + r))
                    out_v[2 * j + c, r * ROWS : (r + 1) * ROWS, lanes] = rows[:, lanes]
            if chunk == CHUNKS - 1:
                place(j).start()

        loop(0, PAIRS_OUT, step)

    def level_two(chunk):
        load_received(recv_a, chunk)
        translate(1)
        assemble(1, chunk)
        send(1, chunk)

    def level_three(chunk):
        load_received(recv_b, chunk)
        translate(2)

    table_copies[0].wait()
    for copy in first_in:
        copy.wait()
    for copy in late_in:
        copy.start()
    translate(0)
    assemble(0, 0)
    pl.semaphore_wait(barrier, 2 * (GROUP - 1))
    send(0, 0)
    loop(1, GROUP, lambda d: owner_copy(d).start())
    list_of(1)
    list_of(2)
    tables[3, 0:1, 0:PAIRS] = send_table(own_in[...])
    table_copies[3].start()
    for chunk in range(1, CHUNKS):
        assemble(0, chunk)
    for copy in table_copies[1:4]:
        copy.wait()
    for copy in late_in:
        copy.wait()
    loop(1, GROUP, lambda d: owner_copy(d).wait())
    tables[4, 0:1, 0:PAIRS] = arrival_table(own_all[:, 0, 0:BOX], w)
    arrival_copy.start()
    arrival_copy.wait()

    sent(0, 0)
    send(0, 1)
    arrive(0, 0)
    level_two(0)
    sent(0, 1)
    send(0, 2)
    arrive(0, 1)
    level_two(1)
    arrive(1, 0)
    level_three(0)
    hand(0, 0, 15)
    keep(0)
    sent(0, 2)
    send(0, 3)
    arrive(0, 2)
    level_two(2)
    arrive(1, 1)
    level_three(1)
    hand(1, 0, 15)
    keep(1)
    arrive(0, 3)
    level_two(3)
    arrive(1, 2)
    level_three(2)
    hand(2, 0, 15)
    keep(2)
    arrive(1, 3)
    level_three(3)
    hand(3, 0, 15)
    keep(3)
    sent(0, 3)

    for chunk in range(CHUNKS):
        sent(1, chunk)
    for chunk in range(CHUNKS):
        arrive(2, chunk)
        finish(chunk)
    loop(0, PAIRS_OUT, lambda j: place(j).wait())
    for chunk in range(CHUNKS):
        sent(2, chunk)


def per_device(charges, pairs_a, pairs_b, pairs_c, mats_a, mats_b, mats_c, box_owner):
    in_hbm = pl.BlockSpec(memory_space=pltpu.HBM)
    flops = 2 * 3 * PAIRS * R * R * RHS
    return pl.pallas_call(
        body,
        out_shape=jax.ShapeDtypeStruct(charges.shape, charges.dtype),
        in_specs=[in_hbm] * 8,
        out_specs=in_hbm,
        scratch_shapes=[
            pltpu.VMEM((BOX, R, RHS), BF),
            *[pltpu.VMEM((TRANS, R, R), BF)] * 3,
            pltpu.VMEM((3, 4, PAIRS), jnp.int32),
            pltpu.VMEM((1, BOX), jnp.int32),
            pltpu.VMEM((GROUP, 8, 128), jnp.int32),
            pltpu.VMEM((5, 8, 128), jnp.int32),
            pltpu.SMEM((4, 8, 128), jnp.int32),
            pltpu.SMEM((8, 128), jnp.int32),
            pltpu.VMEM((BOX, R, RHS), BF),
            pltpu.VMEM((PAIRS + 1, R, RHS), BF),
            *[pltpu.VMEM((CHUNKS, GROUP, TILES, PIECE, RHS), BF)] * 4,
            pltpu.VMEM((CHUNKS, GROUP, ROWS, RHS), BF),
            *[pltpu.VMEM((GROUP, ROWS, RHS), BF)] * CHUNKS,
            pltpu.VMEM((BOX, R, RHS), BF),
            pltpu.SemaphoreType.DMA((2, SPLIT)),
            pltpu.SemaphoreType.DMA((2,)),
            pltpu.SemaphoreType.DMA((4,)),
            pltpu.SemaphoreType.DMA((5,)),
            pltpu.SemaphoreType.DMA((PAIRS_OUT,)),
            pltpu.SemaphoreType.DMA((GROUP,)),
            pltpu.SemaphoreType.DMA((GROUP,)),
            pltpu.SemaphoreType.DMA((3, CHUNKS, GROUP)),
            pltpu.SemaphoreType.DMA((3, CHUNKS, GROUP)),
        ],
        compiler_params=pltpu.CompilerParams(
            collective_id=0, has_side_effects=True, vmem_limit_bytes=62 << 20
        ),
        cost_estimate=pl.CostEstimate(flops=flops, bytes_accessed=5 << 20, transcendentals=0),
        name="butterfly",
    )(
        charges,
        pairs_a.T,
        pairs_b.T,
        pairs_c.T,
        mats_a,
        mats_b,
        mats_c,
        box_owner.reshape(1, BOX),
    )


def solution(mesh):
    both = ("wide", "narrow")
    placed = (
        P(both, None, None),
        P(both, None),
        P(both, None),
        P(both, None),
        P(both, None, None),
        P(both, None, None),
        P(both, None, None),
        P("wide", "narrow", None),
    )
    return jax.shard_map(
        per_device,
        mesh=mesh,
        in_specs=placed,
        out_specs=P(both, None, None),
        check_vma=False,
    )
```

```python
import functools

import jax
import jax.numpy as jnp
from jax import lax
from jax.experimental import pallas as pl
from jax.experimental.pallas import tpu as pltpu
from jax.sharding import PartitionSpec as P

MESH = pl.DeviceIdType.MESH
R = 256
RHS = 128
BOX = 16
PAIRS = 64
TRANS = 8
GROUP = 16
PIECE = R // GROUP
CHUNKS = 4
LANES = RHS // CHUNKS
TILES = BOX // CHUNKS
PARTS = CHUNKS // 2
ROWS = R // PARTS
PAIRS_OUT = BOX // 2
SPLIT = 4
UNROLL = 32
BF = jnp.bfloat16
F32 = jnp.float32


def far_first(e):
    return 8 + jnp.where(lax.rem(e, 2) == 1, -((e + 1) // 2), e // 2)


FAR_FIRST = tuple(
    4 * dy + dx
    for dy, dx in (
        (2, 2), (2, 3), (2, 1), (3, 2), (1, 2), (3, 1), (1, 3), (3, 3),
        (1, 1), (2, 0), (0, 2), (3, 0), (1, 0), (0, 3), (0, 1),
    )
)


def torus_far_first(e):
    low = sum(d << (4 * i) for i, d in enumerate(FAR_FIRST[:7]))
    high = sum(d << (4 * i) for i, d in enumerate(FAR_FIRST[7:14]))
    first = (jnp.int32(low) >> (4 * jnp.minimum(e, 6))) & 15
    later = (jnp.int32(high) >> (4 * jnp.clip(e - 7, 0, 6))) & 15
    return jnp.where(e < 7, first, jnp.where(e < 14, later, FAR_FIRST[14]))


def on_torus(w, d):
    return ((w // 4 + d // 4) & 3) * 4 + ((w + d) & 3)


def column_of(row, eye):
    return jnp.sum(jnp.where(eye, row, 0), axis=1, keepdims=True)


def list_table(rows, tiled):
    line = lax.broadcasted_iota(jnp.int32, (PAIRS, PAIRS), 0)
    lane = lax.broadcasted_iota(jnp.int32, (PAIRS, PAIRS), 1)
    eye = line == lane
    source, target, matrix, live = (rows[i : i + 1, :] for i in range(4))
    place = lax.broadcasted_iota(jnp.int32, (1, PAIRS), 1)
    group = jnp.where(live > 0, target, BOX)
    key = group * PAIRS + place
    turn = (target - source) & (CHUNKS - 1)
    place_of = source // CHUNKS + TILES * turn if tiled else source
    word = place_of | (matrix << 4)
    key_col = column_of(key, eye)
    word_col = column_of(word, eye)
    group_col = key_col // PAIRS
    before = key < key_col
    rank_col = jnp.sum(jnp.where(before, 1, 0), axis=1, keepdims=True)
    follows = jnp.sum(jnp.where(before & (group == group_col), 1, 0), axis=1, keepdims=True)
    word_col = word_col | jnp.where((follows > 0) & (group_col < BOX), 1 << 7, 0)
    ordered = jnp.sum(jnp.where(rank_col == lane, word_col, 0), axis=0, keepdims=True)
    upto = jnp.sum(jnp.where(group_col <= lane, 1, 0), axis=0, keepdims=True)
    count = jnp.sum(jnp.where(group_col == lane, 1, 0), axis=0, keepdims=True)
    last = jnp.where(count > 0, upto - 1, PAIRS)
    return ordered, last


def send_table(row):
    line = lax.broadcasted_iota(jnp.int32, (BOX, BOX), 0)
    lane = lax.broadcasted_iota(jnp.int32, (BOX, BOX), 1)
    eye = line == lane
    col = column_of(row, eye)
    earlier = jnp.sum(jnp.where((row == col) & (lane < line), 1, 0), axis=1, keepdims=True)
    slot = 2 * col + earlier
    wide = lax.broadcasted_iota(jnp.int32, (BOX, PAIRS), 1)
    box = lax.broadcasted_iota(jnp.int32, (BOX, PAIRS), 0)
    return jnp.sum(jnp.where(slot == wide, box, 0), axis=0, keepdims=True)


def arrival_table(owners, me):
    hands = jnp.sum(jnp.where(owners == me, 1, 0), axis=1, keepdims=True)
    line = lax.broadcasted_iota(jnp.int32, (GROUP, GROUP), 0)
    lane = lax.broadcasted_iota(jnp.int32, (GROUP, GROUP), 1)
    filled = jnp.where(hands > 0, 1, 0)
    filled_row = jnp.sum(jnp.where(line == lane, filled, 0), axis=0, keepdims=True)
    rank = jnp.sum(jnp.where(lane < line, filled_row, 0), axis=1, keepdims=True)
    wide = lax.broadcasted_iota(jnp.int32, (GROUP, PAIRS), 1)
    index = lax.broadcasted_iota(jnp.int32, (GROUP, PAIRS), 0)
    return jnp.sum(jnp.where((filled > 0) & (rank == wide), index, 0), axis=0, keepdims=True)


def turned(x, groups):
    if isinstance(groups, int):
        return x if groups % CHUNKS == 0 else pltpu.roll(x, (groups % CHUNKS) * LANES, 1)
    return pltpu.roll(x, (groups & (CHUNKS - 1)) * LANES, 1)


def body(
    charges, pairs_a, pairs_b, pairs_c, mats_a, mats_b, mats_c, owner, out,
    c_v, m_a, m_b, m_c, lists, own_in, own_all, tables, table_s, arrival_s,
    x_v, p_v, stage_a, recv_a, stage_b, recv_b, stage_c, *rest,
):
    recv_c = rest[:CHUNKS]
    in_sem, late_sem, small_sem, table_sem, own_send, own_recv, send_sem, recv_sem = rest[CHUNKS:]
    w = lax.axis_index("wide")
    n = lax.axis_index("narrow")
    barrier = pltpu.get_barrier_semaphore()

    def greet(d, carry):
        pl.semaphore_signal(
            barrier, inc=1, device_id=(w, lax.rem(n + d, GROUP)), device_id_type=MESH
        )
        pl.semaphore_signal(
            barrier, inc=1, device_id=(lax.rem(w + d, GROUP), n), device_id_type=MESH
        )
        return carry

    small = [
        pltpu.make_async_copy(src, lists.at[i], small_sem.at[i])
        for i, src in enumerate((pairs_a, pairs_b, pairs_c))
    ]
    small.append(pltpu.make_async_copy(owner, own_in, small_sem.at[3]))
    first_in = []
    for i, (src, dst) in enumerate(((charges, c_v), (mats_a, m_a))):
        size = src.shape[0] // SPLIT
        for k in range(SPLIT):
            span = pl.ds(k * size, size)
            first_in.append(
                pltpu.make_async_copy(src.at[span], dst.at[span], in_sem.at[i, k])
            )
    late_in = [
        pltpu.make_async_copy(mats_b, m_b, late_sem.at[0]),
        pltpu.make_async_copy(mats_c, m_c, late_sem.at[1]),
    ]
    for copy in small:
        copy.start()
    for copy in first_in:
        copy.start()
    lax.fori_loop(1, GROUP, greet, 0)

    table_copies = [
        pltpu.make_async_copy(tables.at[i], table_s.at[i], table_sem.at[i]) for i in range(4)
    ]
    arrival_copy = pltpu.make_async_copy(tables.at[4], arrival_s, table_sem.at[4])
    for copy in small:
        copy.wait()

    def list_of(level):
        ordered, last = list_table(lists[level], level > 0)
        tables[level, 0:1, 0:PAIRS] = ordered
        tables[level, 1:2, 0:PAIRS] = last
        table_copies[level].start()

    list_of(0)
    own_all[w] = jnp.full((8, 128), -1, jnp.int32)
    own_all[w, 0:1, 0:BOX] = own_in[...]
    p_v[PAIRS] = jnp.zeros((R, RHS), BF)
    group = lax.broadcasted_iota(jnp.int32, (R, RHS), 1) // LANES

    def side_by_side(parts):
        tile = parts[0]
        for g in range(1, CHUNKS):
            tile = jnp.where(group[: tile.shape[0]] == g, parts[g], tile)
        return tile

    def narrow_copy(chunk, d):
        to = lax.rem(n + d, GROUP)
        return pltpu.make_async_remote_copy(
            src_ref=stage_a.at[chunk, to],
            dst_ref=recv_a.at[chunk, n],
            send_sem=send_sem.at[0, chunk, d],
            recv_sem=recv_sem.at[0, chunk, d],
            device_id=(w, to),
            device_id_type=MESH,
        )

    def wide_copy(phase, chunk, d):
        to = on_torus(w, d)
        stage, recv = ((stage_b, recv_b.at[chunk]), (stage_c, recv_c[chunk]))[phase - 1]
        return pltpu.make_async_remote_copy(
            src_ref=stage.at[chunk, to],
            dst_ref=recv.at[w],
            send_sem=send_sem.at[phase, chunk, d],
            recv_sem=recv_sem.at[phase, chunk, d],
            device_id=(to, n),
            device_id_type=MESH,
        )

    copies = (
        narrow_copy,
        functools.partial(wide_copy, 1),
        functools.partial(wide_copy, 2),
    )

    def owner_copy(d):
        to = lax.rem(w + d, GROUP)
        return pltpu.make_async_remote_copy(
            src_ref=own_all.at[w],
            dst_ref=own_all.at[w],
            send_sem=own_send.at[d],
            recv_sem=own_recv.at[d],
            device_id=(to, n),
            device_id_type=MESH,
        )

    def loop(low, high, step):
        def one(i, carry):
            step(i)
            return carry

        lax.fori_loop(low, high, one, 0)

    def load_received(recv, chunk):
        def step(i):
            tile = recv[chunk, :, i].reshape(R, RHS)
            for v in range(CHUNKS):
                x_v[v * TILES + i] = turned(tile, v)

        loop(0, TILES, step)

    def translate(level):
        matrices = (m_a, m_b, m_c)[level]
        sources = c_v if level == 0 else x_v

        def one(r, acc):
            word = table_s[level, 0, r]
            product = jnp.dot(
                matrices[(word >> 4) & 7], sources[word & 15], preferred_element_type=F32
            )
            acc = jnp.where((word >> 7) & 1 == 1, acc, 0.0) + product
            p_v[r] = acc.astype(BF)
            return acc

        lax.fori_loop(0, PAIRS, one, jnp.zeros((R, RHS), F32), unroll=UNROLL)

    def assemble(level, chunk):
        stage = (stage_a, stage_b)[level]

        def step(i):
            parts = []
            for g in range(CHUNKS):
                box = p_v[table_s[level, 1, CHUNKS * i + g]]
                parts.append(turned(box, g - chunk) if level == 0 else box)
            stage[chunk, :, i] = side_by_side(parts).reshape(GROUP, PIECE, RHS)

        loop(0, TILES, step)

    def send(level, chunk):
        loop(0, GROUP - 1, lambda e: copies[level](chunk, far_first(e) if level == 0 else torus_far_first(e)).start())
        if level == 0:
            recv_a[chunk, n] = stage_a[chunk, n]
        else:
            recv_b[chunk, w] = stage_b[chunk, w]

    def arrive(level, chunk):
        loop(1, GROUP, lambda d: copies[level](chunk, d).wait_recv())

    def sent(level, chunk):
        loop(1, GROUP, lambda d: copies[level](chunk, d).wait_send())

    def packet(chunk, to):
        parts = []
        for c in range(2):
            box = table_s[3, 0, 2 * to + c]
            slot = table_s[2, 1, box]
            for r in range(PARTS):
                rows = p_v[slot, r * ROWS : (r + 1) * ROWS]
                parts.append(turned(rows, c * PARTS + r - box))
        stage_c[chunk, to] = side_by_side(parts)

    def hand(chunk):
        def step(e):
            d = torus_far_first(e)
            packet(chunk, on_torus(w, d))
            copies[2](chunk, d).start()

        loop(0, GROUP - 1, step)
        packet(chunk, w)
        recv_c[chunk][w] = stage_c[chunk, w]

    def finish(chunk):
        def step(j):
            packed = recv_c[chunk][arrival_s[0, j]]
            lanes = slice(chunk * LANES, (chunk + 1) * LANES)
            for c in range(2):
                for r in range(PARTS):
                    rows = turned(packed, chunk - (c * PARTS + r))
                    out[2 * j + c, r * ROWS : (r + 1) * ROWS, lanes] = rows[:, lanes]

        loop(0, PAIRS_OUT, step)

    def level_two(chunk):
        load_received(recv_a, chunk)
        translate(1)
        assemble(1, chunk)
        send(1, chunk)

    def level_three(chunk):
        load_received(recv_b, chunk)
        translate(2)

    table_copies[0].wait()
    for copy in first_in:
        copy.wait()
    for copy in late_in:
        copy.start()
    translate(0)
    assemble(0, 0)
    pl.semaphore_wait(barrier, 2 * (GROUP - 1))
    send(0, 0)
    loop(1, GROUP, lambda d: owner_copy(d).start())
    list_of(1)
    list_of(2)
    tables[3, 0:1, 0:PAIRS] = send_table(own_in[...])
    table_copies[3].start()
    for chunk in range(1, CHUNKS):
        assemble(0, chunk)
    for copy in table_copies[1:4]:
        copy.wait()
    for copy in late_in:
        copy.wait()
    loop(1, GROUP, lambda d: owner_copy(d).wait())
    tables[4, 0:1, 0:PAIRS] = arrival_table(own_all[:, 0, 0:BOX], w)
    arrival_copy.start()
    arrival_copy.wait()

    sent(0, 0)
    send(0, 1)
    arrive(0, 0)
    level_two(0)
    sent(0, 1)
    send(0, 2)
    arrive(0, 1)
    level_two(1)
    arrive(1, 0)
    level_three(0)
    hand(0)
    sent(0, 2)
    send(0, 3)
    arrive(0, 2)
    level_two(2)
    arrive(1, 1)
    level_three(1)
    hand(1)
    arrive(0, 3)
    level_two(3)
    arrive(1, 2)
    level_three(2)
    hand(2)
    arrive(1, 3)
    level_three(3)
    hand(3)
    sent(0, 3)

    for chunk in range(CHUNKS):
        sent(1, chunk)
    for chunk in range(CHUNKS):
        arrive(2, chunk)
        finish(chunk)
        sent(2, chunk)


def per_device(charges, pairs_a, pairs_b, pairs_c, mats_a, mats_b, mats_c, box_owner):
    in_hbm = pl.BlockSpec(memory_space=pltpu.HBM)
    flops = 2 * 3 * PAIRS * R * R * RHS
    return pl.pallas_call(
        body,
        out_shape=jax.ShapeDtypeStruct(charges.shape, charges.dtype),
        in_specs=[in_hbm] * 8,
        out_specs=pl.BlockSpec(memory_space=pltpu.VMEM),
        scratch_shapes=[
            pltpu.VMEM((BOX, R, RHS), BF),
            *[pltpu.VMEM((TRANS, R, R), BF)] * 3,
            pltpu.VMEM((3, 4, PAIRS), jnp.int32),
            pltpu.VMEM((1, BOX), jnp.int32),
            pltpu.VMEM((GROUP, 8, 128), jnp.int32),
            pltpu.VMEM((5, 8, 128), jnp.int32),
            pltpu.SMEM((4, 8, 128), jnp.int32),
            pltpu.SMEM((8, 128), jnp.int32),
            pltpu.VMEM((BOX, R, RHS), BF),
            pltpu.VMEM((PAIRS + 1, R, RHS), BF),
            *[pltpu.VMEM((CHUNKS, GROUP, TILES, PIECE, RHS), BF)] * 4,
            pltpu.VMEM((CHUNKS, GROUP, ROWS, RHS), BF),
            *[pltpu.VMEM((GROUP, ROWS, RHS), BF)] * CHUNKS,
            pltpu.SemaphoreType.DMA((2, SPLIT)),
            pltpu.SemaphoreType.DMA((2,)),
            pltpu.SemaphoreType.DMA((4,)),
            pltpu.SemaphoreType.DMA((5,)),
            pltpu.SemaphoreType.DMA((GROUP,)),
            pltpu.SemaphoreType.DMA((GROUP,)),
            pltpu.SemaphoreType.DMA((3, CHUNKS, GROUP)),
            pltpu.SemaphoreType.DMA((3, CHUNKS, GROUP)),
        ],
        compiler_params=pltpu.CompilerParams(
            collective_id=0, has_side_effects=True, vmem_limit_bytes=50 << 20
        ),
        cost_estimate=pl.CostEstimate(flops=flops, bytes_accessed=5 << 20, transcendentals=0),
        name="butterfly",
    )(
        pltpu.with_memory_space_constraint(charges, pltpu.HBM),
        pltpu.with_memory_space_constraint(pairs_a.T, pltpu.HBM),
        pltpu.with_memory_space_constraint(pairs_b.T, pltpu.HBM),
        pltpu.with_memory_space_constraint(pairs_c.T, pltpu.HBM),
        pltpu.with_memory_space_constraint(mats_a, pltpu.HBM),
        pltpu.with_memory_space_constraint(mats_b, pltpu.HBM),
        pltpu.with_memory_space_constraint(mats_c, pltpu.HBM),
        pltpu.with_memory_space_constraint(box_owner.reshape(1, BOX), pltpu.HBM),
    )


def solution(mesh):
    both = ("wide", "narrow")
    placed = (
        P(both, None, None),
        P(both, None),
        P(both, None),
        P(both, None),
        P(both, None, None),
        P(both, None, None),
        P(both, None, None),
        P("wide", "narrow", None),
    )
    return jax.shard_map(
        per_device,
        mesh=mesh,
        in_specs=placed,
        out_specs=P(both, None, None),
        check_vma=False,
    )
```

```python
import functools

import jax
import jax.numpy as jnp
from jax import lax
from jax.experimental import pallas as pl
from jax.experimental.pallas import tpu as pltpu
from jax.sharding import PartitionSpec as P

MESH = pl.DeviceIdType.MESH
R = 256
RHS = 128
BOX = 16
PAIRS = 64
TRANS = 8
GROUP = 16
PIECE = R // GROUP
CHUNKS = 4
LANES = RHS // CHUNKS
TILES = BOX // CHUNKS
PARTS = CHUNKS // 2
ROWS = R // PARTS
PAIRS_OUT = BOX // 2
SPLIT = 4
UNROLL = 32
BF = jnp.bfloat16
F32 = jnp.float32


def far_first(e):
    return 8 + jnp.where(lax.rem(e, 2) == 1, -((e + 1) // 2), e // 2)


FAR_FIRST = tuple(
    4 * dy + dx
    for dy, dx in (
        (2, 2), (2, 3), (2, 1), (3, 2), (1, 2), (3, 1), (1, 3), (3, 3),
        (1, 1), (2, 0), (0, 2), (3, 0), (1, 0), (0, 3), (0, 1),
    )
)


def torus_far_first(e):
    low = sum(d << (4 * i) for i, d in enumerate(FAR_FIRST[:7]))
    high = sum(d << (4 * i) for i, d in enumerate(FAR_FIRST[7:14]))
    first = (jnp.int32(low) >> (4 * jnp.minimum(e, 6))) & 15
    later = (jnp.int32(high) >> (4 * jnp.clip(e - 7, 0, 6))) & 15
    return jnp.where(e < 7, first, jnp.where(e < 14, later, FAR_FIRST[14]))


def on_torus(w, d):
    return ((w // 4 + d // 4) & 3) * 4 + ((w + d) & 3)


def column_of(row, eye):
    return jnp.sum(jnp.where(eye, row, 0), axis=1, keepdims=True)


def list_table(rows, tiled):
    line = lax.broadcasted_iota(jnp.int32, (PAIRS, PAIRS), 0)
    lane = lax.broadcasted_iota(jnp.int32, (PAIRS, PAIRS), 1)
    eye = line == lane
    source, target, matrix, live = (rows[i : i + 1, :] for i in range(4))
    place = lax.broadcasted_iota(jnp.int32, (1, PAIRS), 1)
    group = jnp.where(live > 0, target, BOX)
    key = group * PAIRS + place
    turn = (target - source) & (CHUNKS - 1)
    place_of = source // CHUNKS + TILES * turn if tiled else source
    word = place_of | (matrix << 4)
    key_col = column_of(key, eye)
    word_col = column_of(word, eye)
    group_col = key_col // PAIRS
    before = key < key_col
    rank_col = jnp.sum(jnp.where(before, 1, 0), axis=1, keepdims=True)
    follows = jnp.sum(jnp.where(before & (group == group_col), 1, 0), axis=1, keepdims=True)
    word_col = word_col | jnp.where((follows > 0) & (group_col < BOX), 1 << 7, 0)
    ordered = jnp.sum(jnp.where(rank_col == lane, word_col, 0), axis=0, keepdims=True)
    upto = jnp.sum(jnp.where(group_col <= lane, 1, 0), axis=0, keepdims=True)
    count = jnp.sum(jnp.where(group_col == lane, 1, 0), axis=0, keepdims=True)
    last = jnp.where(count > 0, upto - 1, PAIRS)
    return ordered, last


def send_table(row):
    line = lax.broadcasted_iota(jnp.int32, (BOX, BOX), 0)
    lane = lax.broadcasted_iota(jnp.int32, (BOX, BOX), 1)
    eye = line == lane
    col = column_of(row, eye)
    earlier = jnp.sum(jnp.where((row == col) & (lane < line), 1, 0), axis=1, keepdims=True)
    slot = 2 * col + earlier
    wide = lax.broadcasted_iota(jnp.int32, (BOX, PAIRS), 1)
    box = lax.broadcasted_iota(jnp.int32, (BOX, PAIRS), 0)
    return jnp.sum(jnp.where(slot == wide, box, 0), axis=0, keepdims=True)


def arrival_table(owners, me):
    hands = jnp.sum(jnp.where(owners == me, 1, 0), axis=1, keepdims=True)
    line = lax.broadcasted_iota(jnp.int32, (GROUP, GROUP), 0)
    lane = lax.broadcasted_iota(jnp.int32, (GROUP, GROUP), 1)
    filled = jnp.where(hands > 0, 1, 0)
    filled_row = jnp.sum(jnp.where(line == lane, filled, 0), axis=0, keepdims=True)
    rank = jnp.sum(jnp.where(lane < line, filled_row, 0), axis=1, keepdims=True)
    wide = lax.broadcasted_iota(jnp.int32, (GROUP, PAIRS), 1)
    index = lax.broadcasted_iota(jnp.int32, (GROUP, PAIRS), 0)
    return jnp.sum(jnp.where((filled > 0) & (rank == wide), index, 0), axis=0, keepdims=True)


def turned(x, groups):
    if isinstance(groups, int):
        return x if groups % CHUNKS == 0 else pltpu.roll(x, (groups % CHUNKS) * LANES, 1)
    return pltpu.roll(x, (groups & (CHUNKS - 1)) * LANES, 1)


def body(
    charges, pairs_a, pairs_b, pairs_c, mats_a, mats_b, mats_c, owner, out,
    c_v, m_a, m_b, m_c, lists, own_in, own_all, tables, table_s, arrival_s,
    x_v, p_v, stage_a, recv_a, stage_b, recv_b, stage_c, *rest,
):
    recv_c = rest[:CHUNKS]
    in_sem, late_sem, small_sem, table_sem, own_send, own_recv, send_sem, recv_sem = rest[CHUNKS:]
    w = lax.axis_index("wide")
    n = lax.axis_index("narrow")
    barrier = pltpu.get_barrier_semaphore()

    def greet(d, carry):
        pl.semaphore_signal(
            barrier, inc=1, device_id=(w, lax.rem(n + d, GROUP)), device_id_type=MESH
        )
        pl.semaphore_signal(
            barrier, inc=1, device_id=(lax.rem(w + d, GROUP), n), device_id_type=MESH
        )
        return carry

    small = [
        pltpu.make_async_copy(src, lists.at[i], small_sem.at[i])
        for i, src in enumerate((pairs_a, pairs_b, pairs_c))
    ]
    small.append(pltpu.make_async_copy(owner, own_in, small_sem.at[3]))
    first_in = []
    for i, (src, dst) in enumerate(((charges, c_v), (mats_a, m_a))):
        size = src.shape[0] // SPLIT
        for k in range(SPLIT):
            span = pl.ds(k * size, size)
            first_in.append(
                pltpu.make_async_copy(src.at[span], dst.at[span], in_sem.at[i, k])
            )
    late_in = [
        pltpu.make_async_copy(mats_b, m_b, late_sem.at[0]),
        pltpu.make_async_copy(mats_c, m_c, late_sem.at[1]),
    ]
    for copy in small:
        copy.start()
    for copy in first_in:
        copy.start()
    lax.fori_loop(1, GROUP, greet, 0)

    table_copies = [
        pltpu.make_async_copy(tables.at[i], table_s.at[i], table_sem.at[i]) for i in range(4)
    ]
    arrival_copy = pltpu.make_async_copy(tables.at[4], arrival_s, table_sem.at[4])
    for copy in small:
        copy.wait()

    def list_of(level):
        ordered, last = list_table(lists[level], level > 0)
        tables[level, 0:1, 0:PAIRS] = ordered
        tables[level, 1:2, 0:PAIRS] = last
        table_copies[level].start()

    list_of(0)
    own_all[w] = jnp.full((8, 128), -1, jnp.int32)
    own_all[w, 0:1, 0:BOX] = own_in[...]
    p_v[PAIRS] = jnp.zeros((R, RHS), BF)
    group = lax.broadcasted_iota(jnp.int32, (R, RHS), 1) // LANES

    def side_by_side(parts):
        tile = parts[0]
        for g in range(1, CHUNKS):
            tile = jnp.where(group[: tile.shape[0]] == g, parts[g], tile)
        return tile

    def narrow_copy(chunk, d):
        to = lax.rem(n + d, GROUP)
        return pltpu.make_async_remote_copy(
            src_ref=stage_a.at[chunk, to],
            dst_ref=recv_a.at[chunk, n],
            send_sem=send_sem.at[0, chunk, d],
            recv_sem=recv_sem.at[0, chunk, d],
            device_id=(w, to),
            device_id_type=MESH,
        )

    def wide_copy(phase, chunk, d):
        to = on_torus(w, d)
        stage, recv = ((stage_b, recv_b.at[chunk]), (stage_c, recv_c[chunk]))[phase - 1]
        return pltpu.make_async_remote_copy(
            src_ref=stage.at[chunk, to],
            dst_ref=recv.at[w],
            send_sem=send_sem.at[phase, chunk, d],
            recv_sem=recv_sem.at[phase, chunk, d],
            device_id=(to, n),
            device_id_type=MESH,
        )

    copies = (
        narrow_copy,
        functools.partial(wide_copy, 1),
        functools.partial(wide_copy, 2),
    )

    def owner_copy(d):
        to = lax.rem(w + d, GROUP)
        return pltpu.make_async_remote_copy(
            src_ref=own_all.at[w],
            dst_ref=own_all.at[w],
            send_sem=own_send.at[d],
            recv_sem=own_recv.at[d],
            device_id=(to, n),
            device_id_type=MESH,
        )

    def loop(low, high, step):
        def one(i, carry):
            step(i)
            return carry

        lax.fori_loop(low, high, one, 0)

    def load_received(recv, chunk):
        def step(i):
            tile = recv[chunk, :, i].reshape(R, RHS)
            for v in range(CHUNKS):
                x_v[v * TILES + i] = turned(tile, v)

        loop(0, TILES, step)

    def translate(level):
        matrices = (m_a, m_b, m_c)[level]
        sources = c_v if level == 0 else x_v

        def one(r, acc):
            word = table_s[level, 0, r]
            product = jnp.dot(
                matrices[(word >> 4) & 7], sources[word & 15], preferred_element_type=F32
            )
            acc = jnp.where((word >> 7) & 1 == 1, acc, 0.0) + product
            p_v[r] = acc.astype(BF)
            return acc

        lax.fori_loop(0, PAIRS, one, jnp.zeros((R, RHS), F32), unroll=UNROLL)

    def assemble(level, chunk):
        stage = (stage_a, stage_b)[level]

        def step(i):
            parts = []
            for g in range(CHUNKS):
                box = p_v[table_s[level, 1, CHUNKS * i + g]]
                parts.append(turned(box, g - chunk) if level == 0 else box)
            stage[chunk, :, i] = side_by_side(parts).reshape(GROUP, PIECE, RHS)

        loop(0, TILES, step)

    def send(level, chunk):
        loop(0, GROUP - 1, lambda e: copies[level](chunk, far_first(e) if level == 0 else torus_far_first(e)).start())
        if level == 0:
            recv_a[chunk, n] = stage_a[chunk, n]
        else:
            recv_b[chunk, w] = stage_b[chunk, w]

    def arrive(level, chunk):
        loop(1, GROUP, lambda d: copies[level](chunk, d).wait_recv())

    def sent(level, chunk):
        loop(1, GROUP, lambda d: copies[level](chunk, d).wait_send())

    def packet(chunk, to):
        parts = []
        for c in range(2):
            box = table_s[3, 0, 2 * to + c]
            slot = table_s[2, 1, box]
            for r in range(PARTS):
                rows = p_v[slot, r * ROWS : (r + 1) * ROWS]
                parts.append(turned(rows, c * PARTS + r - box))
        stage_c[chunk, to] = side_by_side(parts)

    def hand(chunk):
        def step(e):
            d = torus_far_first(e)
            packet(chunk, on_torus(w, d))
            copies[2](chunk, d).start()

        loop(0, GROUP - 1, step)
        packet(chunk, w)
        recv_c[chunk][w] = stage_c[chunk, w]

    def finish(chunk):
        def step(j):
            packed = recv_c[chunk][arrival_s[0, j]]
            lanes = slice(chunk * LANES, (chunk + 1) * LANES)
            for c in range(2):
                for r in range(PARTS):
                    rows = turned(packed, chunk - (c * PARTS + r))
                    out[2 * j + c, r * ROWS : (r + 1) * ROWS, lanes] = rows[:, lanes]

        loop(0, PAIRS_OUT, step)

    def level_two(chunk):
        load_received(recv_a, chunk)
        translate(1)
        assemble(1, chunk)
        send(1, chunk)

    def level_three(chunk):
        load_received(recv_b, chunk)
        translate(2)

    table_copies[0].wait()
    for copy in first_in:
        copy.wait()
    for copy in late_in:
        copy.start()
    translate(0)
    assemble(0, 0)
    pl.semaphore_wait(barrier, 2 * (GROUP - 1))
    send(0, 0)
    loop(1, GROUP, lambda d: owner_copy(d).start())
    list_of(1)
    list_of(2)
    tables[3, 0:1, 0:PAIRS] = send_table(own_in[...])
    table_copies[3].start()
    for chunk in range(1, CHUNKS):
        assemble(0, chunk)
    for copy in table_copies[1:4]:
        copy.wait()
    for copy in late_in:
        copy.wait()
    loop(1, GROUP, lambda d: owner_copy(d).wait())
    tables[4, 0:1, 0:PAIRS] = arrival_table(own_all[:, 0, 0:BOX], w)
    arrival_copy.start()
    arrival_copy.wait()

    sent(0, 0)
    send(0, 1)
    arrive(0, 0)
    level_two(0)
    sent(0, 1)
    send(0, 2)
    arrive(0, 1)
    level_two(1)
    arrive(1, 0)
    level_three(0)
    sent(0, 2)
    send(0, 3)
    hand(0)
    arrive(0, 2)
    level_two(2)
    arrive(1, 1)
    level_three(1)
    hand(1)
    arrive(0, 3)
    level_two(3)
    arrive(1, 2)
    level_three(2)
    hand(2)
    arrive(1, 3)
    level_three(3)
    hand(3)
    sent(0, 3)

    for chunk in range(CHUNKS):
        sent(1, chunk)
    for chunk in range(CHUNKS):
        arrive(2, chunk)
        finish(chunk)
        sent(2, chunk)


def per_device(charges, pairs_a, pairs_b, pairs_c, mats_a, mats_b, mats_c, box_owner):
    in_hbm = pl.BlockSpec(memory_space=pltpu.HBM)
    flops = 2 * 3 * PAIRS * R * R * RHS
    return pl.pallas_call(
        body,
        out_shape=jax.ShapeDtypeStruct(charges.shape, charges.dtype),
        in_specs=[in_hbm] * 8,
        out_specs=pl.BlockSpec(memory_space=pltpu.VMEM),
        scratch_shapes=[
            pltpu.VMEM((BOX, R, RHS), BF),
            *[pltpu.VMEM((TRANS, R, R), BF)] * 3,
            pltpu.VMEM((3, 4, PAIRS), jnp.int32),
            pltpu.VMEM((1, BOX), jnp.int32),
            pltpu.VMEM((GROUP, 8, 128), jnp.int32),
            pltpu.VMEM((5, 8, 128), jnp.int32),
            pltpu.SMEM((4, 8, 128), jnp.int32),
            pltpu.SMEM((8, 128), jnp.int32),
            pltpu.VMEM((BOX, R, RHS), BF),
            pltpu.VMEM((PAIRS + 1, R, RHS), BF),
            *[pltpu.VMEM((CHUNKS, GROUP, TILES, PIECE, RHS), BF)] * 4,
            pltpu.VMEM((CHUNKS, GROUP, ROWS, RHS), BF),
            *[pltpu.VMEM((GROUP, ROWS, RHS), BF)] * CHUNKS,
            pltpu.SemaphoreType.DMA((2, SPLIT)),
            pltpu.SemaphoreType.DMA((2,)),
            pltpu.SemaphoreType.DMA((4,)),
            pltpu.SemaphoreType.DMA((5,)),
            pltpu.SemaphoreType.DMA((GROUP,)),
            pltpu.SemaphoreType.DMA((GROUP,)),
            pltpu.SemaphoreType.DMA((3, CHUNKS, GROUP)),
            pltpu.SemaphoreType.DMA((3, CHUNKS, GROUP)),
        ],
        compiler_params=pltpu.CompilerParams(
            collective_id=0, has_side_effects=True, vmem_limit_bytes=50 << 20
        ),
        cost_estimate=pl.CostEstimate(flops=flops, bytes_accessed=5 << 20, transcendentals=0),
        name="butterfly",
    )(
        pltpu.with_memory_space_constraint(charges, pltpu.HBM),
        pltpu.with_memory_space_constraint(pairs_a.T, pltpu.HBM),
        pltpu.with_memory_space_constraint(pairs_b.T, pltpu.HBM),
        pltpu.with_memory_space_constraint(pairs_c.T, pltpu.HBM),
        pltpu.with_memory_space_constraint(mats_a, pltpu.HBM),
        pltpu.with_memory_space_constraint(mats_b, pltpu.HBM),
        pltpu.with_memory_space_constraint(mats_c, pltpu.HBM),
        pltpu.with_memory_space_constraint(box_owner.reshape(1, BOX), pltpu.HBM),
    )


def solution(mesh):
    both = ("wide", "narrow")
    placed = (
        P(both, None, None),
        P(both, None),
        P(both, None),
        P(both, None),
        P(both, None, None),
        P(both, None, None),
        P(both, None, None),
        P("wide", "narrow", None),
    )
    return jax.shard_map(
        per_device,
        mesh=mesh,
        in_specs=placed,
        out_specs=P(both, None, None),
        check_vma=False,
    )
```
